768 devices in a mesh: lon: 64 (over x, z_hi, y), lat: 12 (over z_lo, core).
Axes of the slice: x: 4, y: 8, z: 12 (z_hi: 2, z_lo: 6; z = z_hi * 6 + z_lo), core: 2. Of those that a mesh axis runs over, the one named last changes fastest.
Arguments:
- fields: bfloat16 [180, 641, 768], P('lat', None, 'lon'), may hold values from -6 to 6
- support: int32 [180, 5], replicated, may hold values from 1 to 48, as said below
- filter_weight: bfloat16 [641, 4], replicated, may hold values from -4 to 4
- w_up: bfloat16 [641, 1282], replicated, may hold values from -0.25 to 0.25
- w_down: bfloat16 [1282, 641], replicated, may hold values from -0.15625 to 0.15625
Outputs:
- result: bfloat16 [180, 641, 768], P('lat', None, 'lon')
The draws below stay inside these ranges and needn't reach their ends.
Inputs may be any that keep to these rules, and one draw needn't show every extreme that they name: support[o, j] is the half-width in longitude cells of the filter's support at output latitude o and latitude offset j - 2; the value 48 occurs.
All inputs are finite; a program needn't handle non-finite values.
Results may differ from the reference program's by a relative error of at most 0.0085.
Values may be sent and summed in bfloat16 or wider, within the bound.
A program may use at most 64 MiB of HBM per device.

```python
import math
import jax
import jax.numpy as jnp
from jax import lax

C = 641
HID = 1282
K = 4
R = 2
NLAT = 180
NLON = 768
WMAX = 48


def draw_support(key, part):
    key_widths = jax.random.fold_in(key, 11)
    key_row = jax.random.fold_in(key, 12)
    key_column = jax.random.fold_in(key, 13)
    widths = jax.random.randint(key_widths, (NLAT, 2 * R + 1), 1, WMAX + 1, dtype=jnp.int32)
    row_pick = jax.random.randint(key_row, (), 0, NLAT, dtype=jnp.int32)
    column_pick = jax.random.randint(key_column, (), 0, 2 * R + 1, dtype=jnp.int32)
    return widths.at[row_pick, column_pick].set(WMAX)


def shard_levels(stream_key, extent, shards, smallest, largest):
    level, own = 1.0, jax.random.fold_in(stream_key, 6)
    for position, shards_of in shards:
        draws = jnp.exp(jax.random.uniform(jax.random.fold_in(own, position), (shards_of,), jnp.float32, smallest / len(shards), largest / len(shards)))
        level = level * jnp.repeat(draws, extent[position] // shards_of).reshape([-1 if axis == position else 1 for axis in range(len(extent))])
    return level


def noise(stream_key, shape, width, reach, shards=(), kind=jnp.bfloat16):
    values = width * jax.random.normal(stream_key, shape, jnp.float32)
    if shards:
        values = values * shard_levels(stream_key, shape, shards, -0.22, 0.18)
    return jnp.clip(values, -reach, reach).astype(kind)


def setup_inputs(seed: int = 0) -> dict:
    streams_of = jax.random.split(jax.random.key(seed), 6)
    fields = noise(streams_of[0], (NLAT, C, NLON), 1.0, 6.0, ((0, 12), (2, 64)))
    support = draw_support(jax.random.fold_in(streams_of[5], 71), 0)
    filter_weight = noise(streams_of[2], (C, K), 1.0, 4.0)
    w_up = noise(streams_of[3], (C, HID), C ** -0.5, 0.25)
    w_down = noise(streams_of[4], (HID, C), HID ** -0.5, 0.15625)
    return dict(fields=fields, support=support, filter_weight=filter_weight, w_up=w_up, w_down=w_down)


def basis_matrix(row_out, support, lat_total, block_len):
    half_len = block_len // 2
    shift_amounts = jnp.arange(2 * R + 1, dtype=jnp.int32) - R
    widths = support[jnp.clip(row_out, 0, lat_total - 1)]
    window = jnp.arange(2 * block_len, dtype=jnp.int32)
    column = jnp.arange(block_len, dtype=jnp.int32)
    lon_offset = window[:, None] - column[None, :] - half_len
    width_grid = widths[:, None, None]
    inside = jnp.abs(lon_offset)[None] <= width_grid
    lat_part = (shift_amounts.astype(jnp.float32) / (R + 1.0))[:, None, None]
    lon_part = lon_offset[None].astype(jnp.float32) / (width_grid + 1).astype(jnp.float32)
    radius = jnp.sqrt(lat_part * lat_part + lon_part * lon_part)
    levels = jnp.arange(K, dtype=jnp.float32)
    hat_values = jnp.maximum(0.0, 1.0 - jnp.abs(radius[:, :, None, :] * (K - 1.0) - levels[None, None, :, None]))
    rows_in = (row_out + shift_amounts).astype(jnp.float32)
    weight = jnp.sin(math.pi * (rows_in + 0.5) / lat_total) / jnp.sqrt((2.0 * R + 1.0) * (2 * widths + 1).astype(jnp.float32))
    basis_table = jnp.where(inside[:, :, None, :], hat_values * weight[:, None, None, None], 0.0)
    return basis_table.reshape(2 * R + 1, 2 * block_len, K * block_len).astype(jnp.bfloat16)

def correlate(source, filter_weights, support, starting_row, out_rows, lat_total):
    line_total, feature_channels, longitude_loop = source.shape
    block_len = min(128, longitude_loop)
    half_len = block_len // 2
    block_count = longitude_loop // block_len
    blocked = source.reshape(line_total, feature_channels, block_count, block_len)
    leading = jnp.roll(blocked, 1, axis=2)[..., half_len:]
    trailing = jnp.roll(blocked, -1, axis=2)[..., :half_len]
    window = jnp.concatenate([leading, blocked, trailing], axis=3)

    def one_row(row_stride):
        picked = lax.dynamic_slice_in_dim(window, row_stride, 2 * R + 1, 0)
        basis_table = basis_matrix(starting_row + row_stride, support, lat_total, block_len)
        weighted_terms = jnp.zeros((feature_channels * block_count, K * block_len), jnp.float32)
        for offset in range(2 * R + 1):
            lhs_rows = picked[offset].reshape(feature_channels * block_count, 2 * block_len)
            weighted_terms = weighted_terms + jnp.dot(lhs_rows, basis_table[offset], preferred_element_type=jnp.float32)
        weighted_terms = weighted_terms.reshape(feature_channels, block_count, K, block_len)
        return jnp.einsum('qgrf,qr->qgf', weighted_terms, filter_weights).reshape(feature_channels, longitude_loop)
    return lax.map(one_row, jnp.arange(out_rows, dtype=jnp.int32))

def feed_forward(combined, w_up, w_down):
    values = combined.astype(jnp.float32)
    row_mean = lax.optimization_barrier(jnp.mean(values, axis=-2, keepdims=True))
    centered = values - row_mean
    spread = lax.optimization_barrier(jnp.mean(centered * centered, axis=-2, keepdims=True))
    normed = (centered * lax.rsqrt(spread + 1e-05)).astype(jnp.bfloat16)
    raised = jnp.einsum('...cn,ch->...hn', normed, w_up, preferred_element_type=jnp.float32)
    hidden = jax.nn.gelu(raised, approximate=False).astype(jnp.bfloat16)
    lowered = jnp.einsum('...hn,hc->...cn', hidden, w_down, preferred_element_type=jnp.float32)
    return (values + lowered).astype(jnp.bfloat16)

def reference(fields, support, filter_weight, w_up, w_down):
    lat_total = fields.shape[0]
    padded = jnp.pad(fields, ((R, R), (0, 0), (0, 0)))
    conv_out = correlate(padded, filter_weight.astype(jnp.float32), support, 0, lat_total, lat_total)
    combined = (fields.astype(jnp.float32) + conv_out).astype(jnp.bfloat16)

    def per_row(row_data):
        return feed_forward(row_data, w_up, w_down)
    return lax.map(per_row, combined)
```

```python
import functools
import math

import jax
import jax.numpy as jnp
import numpy as np
from jax import lax
from jax.experimental import pallas as pl
from jax.experimental.pallas import tpu as pltpu
from jax.sharding import PartitionSpec as P

MESH = pl.DeviceIdType.MESH
NB = 12
ROWS = 15
C = 641
CH = 10
OWN = 64
K = 4
R = 2
F32 = jnp.float32
BF = jnp.bfloat16


def iota(shape, dim):
    return lax.broadcasted_iota(jnp.int32, shape, dim)


def pack(f_ref, o_ref, roll_ref):
    lane = iota((16, 128), 1)
    sub = iota((16, 128), 0)
    for n in range(NB):
        x = f_ref[n].astype(F32)
        x = jnp.concatenate([x, jnp.zeros((ROWS, 768 - C), F32)], axis=1)
        x = jnp.concatenate([x, jnp.zeros((1, 768), F32)], axis=0)
        roll_ref[n] = pltpu.roll(x, CH * n, 1) if n else x
    extra = jnp.zeros((16, 128), F32)
    spread = jnp.zeros((16, 128), F32)
    for n in range(NB):
        start = 640 + CH * n
        col = roll_ref[n, :, pl.ds(start % 768, 1)] if start < 768 else None
        if col is None:
            col = roll_ref[n, :, pl.ds(start - 768, 1)]
        col = jnp.broadcast_to(col, (16, 128))
        if n < 8:
            extra = jnp.where(lane == 120 + n, col, extra)
        else:
            spread = jnp.where(lane == 8 * sub + (n - 8), col, spread)
    spread = jnp.where(sub < ROWS, spread, 0.0)
    last = jnp.sum(spread, axis=0, keepdims=True)
    for p in range(OWN):
        begin = CH * p
        cut = begin % 128
        tile = begin // 128
        here = (lane - cut) & 127
        acc = jnp.zeros((16, 128), F32)
        for n in range(NB):
            lo, hi = begin + CH * n, begin + CH * n + CH
            inside = (here >= CH * n) & (here < CH * n + CH)
            first, final = lo // 128, (hi - 1) // 128
            acc = jnp.where(inside, roll_ref[n, :, pl.ds(first % 6 * 128, 128)], acc) if first == final else jnp.where(
                inside,
                jnp.where(
                    lane >= 64,
                    roll_ref[n, :, pl.ds(first % 6 * 128, 128)],
                    roll_ref[n, :, pl.ds(final % 6 * 128, 128)],
                ),
                acc,
            )
        if cut:
            acc = pltpu.roll(acc, 128 - cut, 1)
        acc = jnp.where(lane >= 120, extra, acc)
        acc = jnp.where(sub == 15, last, acc)
        o_ref[p] = acc.astype(BF)


def unpack(m_ref, c_ref, turn_ref):
    lane = iota((16, 128), 1)
    sub = iota((16, 128), 0)
    for q in range(OWN):
        x = m_ref[q].astype(F32)
        cut = (CH * q) % 128
        turn_ref[q] = pltpu.roll(x, cut, 1) if cut else x
    x0 = m_ref[0].astype(F32)
    row = jnp.broadcast_to(x0[15:16], (16, 128))
    lane1 = iota((16, 128), 1)
    for n in range(NB):
        tiles = []
        for t in range(6):
            acc = jnp.zeros((16, 128), F32)
            for q in range(OWN):
                for lo in (CH * (q + n), CH * (q + n) - 768):
                    a, b = max(lo, t * 128) - t * 128, min(lo + CH, t * 128 + 128) - t * 128
                    if a < b:
                        acc = jnp.where((lane1 >= a) & (lane1 < b), turn_ref[q], acc)
            tiles.append(acc)
        full = jnp.concatenate(tiles, axis=1)
        if n:
            full = pltpu.roll(full, 768 - CH * n, 1)
        if n < 8:
            col = x0[:, 120 + n : 121 + n]
        else:
            col = jnp.sum(jnp.where(lane == 8 * sub + (n - 8), row, 0.0), axis=1, keepdims=True)
        c_ref[pl.ds(16 * n, 16), pl.ds(0, 640)] = full[:, :640]
        c_ref[pl.ds(16 * n, 16), pl.ds(640, 128)] = jnp.where(lane == 0, col, 0.0)


def order_matrix():
    j = np.arange(128)
    g, s = j // 24, j % 24
    c = 2 * g + np.where(s < 8, 0, np.where(s < 16, 1, np.where(s < 20, 0, 1)))
    n = np.where(s < 8, s, np.where(s < 16, s - 8, np.where(s < 20, s - 8, s - 12)))
    src = np.where(j < 120, CH * n + c, j)
    return (src[:, None] == np.arange(128)[None, :]).astype(np.float32)


def back_matrix():
    out = np.zeros((96, 256), np.float32)
    for g in range(5):
        for s in range(16):
            if s < 12:
                out[16 * g + s, CH * s + 2 * g] = 1
            if s < 8 or s >= 12:
                n = s if s < 8 else s - 4
                out[16 * g + s, 128 + CH * n + 2 * g + 1] = 1
    for s in range(8):
        out[80 + s, 120 + s] = 1
    return out


def last_matrix():
    out = np.zeros((256, 128), np.float32)
    for o in range(ROWS):
        for t in range(4):
            out[16 * o + 8 + t, 8 * o + t] = 1
    return out


def sines():
    i = np.arange(192, dtype=np.float64) - R
    return np.sin(np.pi * (i + 0.5) / 180.0).astype(np.float32)[None]


def build_weights(sup_ref, sin_ref, start, t_ref):
    lane = iota((16, 128), 1)
    rlane = lane // 16
    s = lane % 16
    n_in = jnp.where(s < 12, s, s - 4)
    sub = iota((16, 128), 0)
    n_out = jnp.where(sub < 12, sub, sub - 4)
    diff = (n_in - n_out).astype(F32)

    def one(o, carry):
        local = o % 4
        group = o // 4
        row = jnp.minimum(start + o, 179)
        d = rlane - local
        width = jnp.ones((16, 128), F32)
        sine = jnp.zeros((16, 128), F32)
        for j in range(2 * R + 1):
            width = jnp.where(d == j, sup_ref[j, row].astype(F32), width)
            sine = jnp.where(d == j, sin_ref[0, row + j], sine)
        ok = (d >= 0) & (d <= 2 * R)
        scale = jnp.where(ok, sine / jnp.sqrt((2.0 * R + 1.0) * (2.0 * width + 1.0)), 0.0)
        lat = (d - R).astype(F32) / (R + 1.0)
        lat2 = lat * lat
        base = pl.multiple_of(local * 64, 64)
        for step in range(9):
            m = diff + float(12 * (step - 4))
            lon = m / (width + 1.0)
            radius = jnp.sqrt(lat2 + lon * lon) * (K - 1.0)
            w = jnp.where(jnp.abs(m) <= width, scale, 0.0)
            for k in range(K):
                hat = jnp.maximum(0.0, 1.0 - jnp.abs(radius - float(k)))
                t_ref[group, pl.ds(base + 16 * k, 16), pl.ds(128 * step, 128)] = (hat * w).astype(BF)
        return carry

    lax.fori_loop(0, 16, one, 0)


def build_filter(filt_ref, me, w_ref):
    lane = iota((C, 768), 1)
    chan = lane // 64
    want = jnp.where(chan < CH, me * CH + chan, C - 1)
    pick = jnp.where(iota((C, 768), 0) == want, 1.0, 0.0).astype(BF)
    w_ref[...] = jnp.dot(filt_ref[...], pick, preferred_element_type=F32)


NT = (((1,), (1,)), ((), ()))
TN = (((0,), (0,)), ((), ()))


def spread_rows(order_ref, own_ref, up_ref, down_ref, lat, lats, x_ref, d_ref, e_ref, f_ref):
    lane8 = iota((8, 128), 1)
    sub8 = iota((8, 128), 0)
    left = lane8 < 64
    both = (sub8 < 4) == left
    corner = (sub8 < 4) & left
    eye = (iota((128, 128), 0) == iota((128, 128), 1)).astype(F32).astype(BF)
    order = order_ref[...]

    def load(which, rows, first, keep):
        def rowsof(r):
            x = x_ref[pl.ds(r, 64, stride=16), :]
            if keep is not None:
                x = jnp.where(keep, x, 0.0)
            x = x.astype(BF)
            return jnp.concatenate([x, x], axis=0)

        x_ref[...] = which[...].reshape(1024, 128).astype(F32)
        ex = lax.dot_general(eye, rowsof(15), NT, preferred_element_type=F32)
        for i, r in enumerate(rows):
            d_ref[first + i] = lax.dot_general(order, rowsof(r), NT, preferred_element_type=F32)
            e_ref[first + i] = ex[8 * r : 8 * r + 8]

    load(own_ref, range(ROWS), R, None)
    load(up_ref, (13, 14), 0, lat > 0)
    load(down_ref, (0, 1), ROWS + R, lat < lats - 1)
    for step in range(9):
        f_ref[step, pl.ds(304, 16), :] = jnp.zeros((16, 768), BF)

    def one(r, carry):
        at = pl.multiple_of(16 * r, 16)
        for step in range(9):
            shift = (4 - step) % 128
            turned = d_ref[r]
            ex = e_ref[r]
            if shift:
                turned = pltpu.roll(turned, shift, 1)
                ex = pltpu.roll(ex, shift, 1)
            for g in range(6):
                if g < 5:
                    top = jnp.where(left, turned[24 * g : 24 * g + 8], turned[24 * g + 8 : 24 * g + 16])
                    low = jnp.where(both, turned[24 * g + 16 : 24 * g + 24], 0.0)
                else:
                    top = jnp.where(left, turned[120:128], 0.0)
                    low = jnp.where(corner, ex, 0.0)
                f_ref[step, pl.ds(at, 16), pl.ds(128 * g, 128)] = jnp.concatenate([top, low], axis=0).astype(BF)
        return carry

    lax.fori_loop(0, ROWS + 2 * R, one, 0)


def convolve(t_ref, f_ref, w_ref, back_ref, final_ref, acc_ref, x_ref, z_ref, out_ref):
    def group(g, carry):
        at = pl.multiple_of(64 * g, 64)
        for j in range(3):
            rhs = jnp.concatenate([f_ref[step, pl.ds(at, 128), pl.ds(256 * j, 256)] for step in range(9)], axis=0)
            acc_ref[:, pl.ds(256 * j, 256)] = jnp.dot(t_ref[g], rhs, preferred_element_type=F32)
        for o in range(4):
            conv = jnp.zeros((16, 768), F32)
            for k in range(K):
                conv = conv + acc_ref[pl.ds(64 * o + 16 * k, 16), :] * w_ref[pl.ds(k, 1), :]
            centre = f_ref[4, pl.ds(at + 16 * (o + R), 16), :].astype(F32)
            comb = (centre + conv).astype(BF)
            stack = jnp.concatenate([comb[:, 128 * i : 128 * i + 128] for i in range(6)], axis=0)
            moved = lax.dot_general(stack, back_ref[...], TN, preferred_element_type=F32)
            x_ref[pl.ds(4 * g + o, 64, stride=16), :] = moved[:64, :128] + moved[64:, 128:]
            z_ref[pl.ds(at + 16 * o, 16), :] = comb[:, 640:]
        return carry

    lax.fori_loop(0, 4, group, 0)
    last = lax.dot_general(z_ref[...], final_ref[...], TN, preferred_element_type=F32)
    x_ref[pl.ds(15, 64, stride=16), :] = last[:64]
    out_ref[...] = x_ref[...].reshape(64, 16, 128).astype(BF)


def mlp(c_ref, up_ref, down_ref, out_ref):
    lane = iota((192, 768), 1)
    values = c_ref[...]
    mean = jnp.sum(values, axis=1, keepdims=True) * (1.0 / C)
    centered = jnp.where(lane < C, values - mean, 0.0)
    spread = jnp.sum(centered * centered, axis=1, keepdims=True) * (1.0 / C)
    normed = (centered * lax.rsqrt(spread + 1e-05)).astype(BF)[:, :C]
    raised = jnp.dot(normed, up_ref[...], preferred_element_type=F32)
    hidden = (0.5 * raised * (1.0 + lax.erf(raised * math.sqrt(0.5)))).astype(BF)
    lowered = lax.dot_general(hidden, down_ref[...], NT, preferred_element_type=F32)
    result = (values[:, :C] + lowered).astype(BF)
    for n in range(NB):
        out_ref[n] = result[16 * n : 16 * n + ROWS]


def pack_kernel(f_ref, o_ref, roll_ref):
    pack(f_ref, o_ref, roll_ref)


def conv_kernel(lats, own_ref, up_ref, down_ref, sup_ref, sin_ref, filt_ref, order_ref, back_ref, final_ref, out_ref,
                t_ref, w_ref, x_ref, d_ref, e_ref, f_ref, acc_ref, z_ref):
    me = lax.axis_index("lon")
    lat = lax.axis_index("lat")
    build_weights(sup_ref, sin_ref, lat * ROWS, t_ref)
    build_filter(filt_ref, me, w_ref)
    spread_rows(order_ref, own_ref, up_ref, down_ref, lat, lats, x_ref, d_ref, e_ref, f_ref)
    convolve(t_ref, f_ref, w_ref, back_ref, final_ref, acc_ref, x_ref, z_ref, out_ref)


def mlp_kernel(m_ref, up_ref, down_ref, out_ref, turn_ref, c_ref):
    unpack(m_ref, c_ref, turn_ref)
    mlp(c_ref, up_ref, down_ref, out_ref)


def greet(me, lat, lats, halo):
    barrier = pltpu.get_barrier_semaphore()

    def hail(i, carry):
        pl.semaphore_signal(barrier, inc=1, device_id={"lon": lax.rem(me + i, OWN)}, device_id_type=MESH)
        return carry

    lax.fori_loop(1, OWN, hail, 0)
    if not halo:
        pl.semaphore_wait(barrier, OWN - 1)
        return

    @pl.when(lat > 0)
    def _():
        pl.semaphore_signal(barrier, inc=1, device_id={"lat": lat - 1}, device_id_type=MESH)

    @pl.when(lat < lats - 1)
    def _():
        pl.semaphore_signal(barrier, inc=1, device_id={"lat": lat + 1}, device_id_type=MESH)

    pl.semaphore_wait(barrier, OWN - 1 + (lat > 0).astype(jnp.int32) + (lat < lats - 1).astype(jnp.int32))


def exchange(me, src, dst, send_sem, recv_sem, copy_sem):
    def send(i, carry):
        p = lax.rem(me + i, OWN)
        pltpu.make_async_remote_copy(
            src.at[p], dst.at[me], send_sem, recv_sem, device_id={"lon": p}, device_id_type=MESH
        ).start()
        return carry

    lax.fori_loop(1, OWN, send, 0)
    mine = pltpu.make_async_copy(src.at[me], dst.at[me], copy_sem)
    mine.start()
    mine.wait()
    every = pltpu.make_async_remote_copy(
        src.at[pl.ds(0, OWN - 1)], dst.at[pl.ds(0, OWN - 1)], send_sem, recv_sem,
        device_id={"lon": lax.rem(me + 1, OWN)}, device_id_type=MESH,
    )
    every.wait_recv()
    every.wait_send()


def first_exchange(lats, src, own, up, down, send_sem, recv_sem, copy_sem, halo_send, halo_recv):
    me = lax.axis_index("lon")
    lat = lax.axis_index("lat")
    greet(me, lat, lats, True)
    exchange(me, src, own, send_sem, recv_sem, copy_sem)

    def halo(to, dst, i):
        return pltpu.make_async_remote_copy(
            own, dst, halo_send.at[i], halo_recv.at[i], device_id={"lat": to}, device_id_type=MESH
        )

    @pl.when(lat > 0)
    def _():
        halo(lat - 1, down, 0).start()

    @pl.when(lat < lats - 1)
    def _():
        halo(lat + 1, up, 1).start()

    @pl.when(lat > 0)
    def _():
        halo(lat - 1, down, 0).wait_send()
        halo(lat - 1, up, 1).wait_recv()

    @pl.when(lat < lats - 1)
    def _():
        halo(lat + 1, up, 1).wait_send()
        halo(lat + 1, down, 0).wait_recv()


def second_exchange(src, own, send_sem, recv_sem, copy_sem):
    me = lax.axis_index("lon")
    greet(me, None, None, False)
    exchange(me, src, own, send_sem, recv_sem, copy_sem)


VM = pl.BlockSpec(memory_space=pltpu.VMEM)
SM = pl.BlockSpec(memory_space=pltpu.SMEM)
MSG = jax.ShapeDtypeStruct((OWN, 16, 128), BF)


def params(**kw):
    return pltpu.CompilerParams(vmem_limit_bytes=48 << 20, **kw)


def on_device(lats, fields, support, filter_weight, w_up, w_down):
    points = jnp.transpose(fields, (2, 0, 1))
    messages = pl.pallas_call(
        pack_kernel, out_shape=MSG, in_specs=[VM], out_specs=VM,
        scratch_shapes=[pltpu.VMEM((NB, 16, 768), F32)], compiler_params=params(), name="pack",
    )(points)
    dma = pltpu.SemaphoreType.DMA
    own, up, down = pl.pallas_call(
        functools.partial(first_exchange, lats), out_shape=(MSG,) * 3, in_specs=[VM], out_specs=(VM,) * 3,
        scratch_shapes=[dma, dma, dma, dma((2,)), dma((2,))],
        compiler_params=params(collective_id=0, has_side_effects=True), name="to_owners",
    )(messages)
    back = pl.pallas_call(
        functools.partial(conv_kernel, lats), out_shape=MSG,
        in_specs=[VM, VM, VM, SM, SM, VM, VM, VM, VM], out_specs=VM,
        scratch_shapes=[
            pltpu.VMEM((4, 256, 1152), BF), pltpu.VMEM((K, 768), F32), pltpu.VMEM((1024, 128), F32),
            pltpu.VMEM((ROWS + 2 * R, 128, 128), F32), pltpu.VMEM((ROWS + 2 * R, 8, 128), F32),
            pltpu.VMEM((9, 320, 768), BF), pltpu.VMEM((256, 768), F32), pltpu.VMEM((256, 128), BF),
        ],
        compiler_params=params(), name="convolve",
    )(own, up, down, support.T, jnp.asarray(sines()), filter_weight.T, jnp.asarray(order_matrix(), BF),
      jnp.asarray(back_matrix(), BF), jnp.asarray(last_matrix(), BF))
    pieces = pl.pallas_call(
        second_exchange, out_shape=MSG, in_specs=[VM], out_specs=VM, scratch_shapes=[dma, dma, dma],
        compiler_params=params(collective_id=1, has_side_effects=True), name="to_longitudes",
    )(back)
    result = pl.pallas_call(
        mlp_kernel, out_shape=jax.ShapeDtypeStruct((NB, ROWS, C), BF), in_specs=[VM] * 3, out_specs=VM,
        scratch_shapes=[pltpu.VMEM((OWN, 16, 128), F32), pltpu.VMEM((192, 768), F32)],
        compiler_params=params(), name="channels",
    )(pieces, w_up, w_down.T)
    return jnp.transpose(result, (1, 2, 0))


def solution(mesh):
    in_specs = (P("lat", None, "lon"), P(), P(), P(), P())
    out_specs = P("lat", None, "lon")
    return jax.shard_map(
        functools.partial(on_device, mesh.shape["lat"]), mesh=mesh, in_specs=in_specs, out_specs=out_specs,
        check_vma=False,
    )
```

```python
import functools
import math

import jax
import jax.numpy as jnp
import numpy as np
from jax import lax
from jax.experimental import pallas as pl
from jax.experimental.pallas import tpu as pltpu
from jax.sharding import PartitionSpec as P

MESH = pl.DeviceIdType.MESH
NB = 12
ROWS = 15
C = 641
CH = 10
OWN = 64
K = 4
R = 2
F32 = jnp.float32
BF = jnp.bfloat16


def iota(shape, dim):
    return lax.broadcasted_iota(jnp.int32, shape, dim)


def pack(f_ref, o_ref, roll_ref):
    lane = iota((16, 128), 1)
    sub = iota((16, 128), 0)
    for n in range(NB):
        x = f_ref[n].astype(F32)
        x = jnp.concatenate([x, jnp.zeros((ROWS, 768 - C), F32)], axis=1)
        x = jnp.concatenate([x, jnp.zeros((1, 768), F32)], axis=0)
        roll_ref[n] = pltpu.roll(x, CH * n, 1) if n else x
    extra = jnp.zeros((16, 128), F32)
    spread = jnp.zeros((16, 128), F32)
    for n in range(NB):
        start = 640 + CH * n
        col = roll_ref[n, :, pl.ds(start % 768, 1)] if start < 768 else None
        if col is None:
            col = roll_ref[n, :, pl.ds(start - 768, 1)]
        col = jnp.broadcast_to(col, (16, 128))
        if n < 8:
            extra = jnp.where(lane == 120 + n, col, extra)
        else:
            spread = jnp.where(lane == 8 * sub + (n - 8), col, spread)
    spread = jnp.where(sub < ROWS, spread, 0.0)
    last = jnp.sum(spread, axis=0, keepdims=True)
    for p in range(OWN):
        begin = CH * p
        cut = begin % 128
        tile = begin // 128
        here = (lane - cut) & 127
        acc = jnp.zeros((16, 128), F32)
        for n in range(NB):
            lo, hi = begin + CH * n, begin + CH * n + CH
            inside = (here >= CH * n) & (here < CH * n + CH)
            first, final = lo // 128, (hi - 1) // 128
            acc = jnp.where(inside, roll_ref[n, :, pl.ds(first % 6 * 128, 128)], acc) if first == final else jnp.where(
                inside,
                jnp.where(
                    lane >= 64,
                    roll_ref[n, :, pl.ds(first % 6 * 128, 128)],
                    roll_ref[n, :, pl.ds(final % 6 * 128, 128)],
                ),
                acc,
            )
        if cut:
            acc = pltpu.roll(acc, 128 - cut, 1)
        acc = jnp.where(lane >= 120, extra, acc)
        acc = jnp.where(sub == 15, last, acc)
        o_ref[p] = acc.astype(BF)


def unpack(m_ref, c_ref, turn_ref):
    lane = iota((16, 128), 1)
    sub = iota((16, 128), 0)
    for q in range(OWN):
        x = m_ref[q].astype(F32)
        cut = (CH * q) % 128
        turn_ref[q] = pltpu.roll(x, cut, 1) if cut else x
    x0 = m_ref[0].astype(F32)
    row = jnp.broadcast_to(x0[15:16], (16, 128))
    lane1 = iota((16, 128), 1)
    for n in range(NB):
        tiles = []
        for t in range(6):
            acc = jnp.zeros((16, 128), F32)
            for q in range(OWN):
                for lo in (CH * (q + n), CH * (q + n) - 768):
                    a, b = max(lo, t * 128) - t * 128, min(lo + CH, t * 128 + 128) - t * 128
                    if a < b:
                        acc = jnp.where((lane1 >= a) & (lane1 < b), turn_ref[q], acc)
            tiles.append(acc)
        full = jnp.concatenate(tiles, axis=1)
        if n:
            full = pltpu.roll(full, 768 - CH * n, 1)
        if n < 8:
            col = x0[:, 120 + n : 121 + n]
        else:
            col = jnp.sum(jnp.where(lane == 8 * sub + (n - 8), row, 0.0), axis=1, keepdims=True)
        c_ref[pl.ds(16 * n, 16), pl.ds(0, 640)] = full[:, :640]
        c_ref[pl.ds(16 * n, 16), pl.ds(640, 128)] = jnp.where(lane == 0, col, 0.0)


def order_matrix():
    j = np.arange(128)
    g, s = j // 24, j % 24
    c = 2 * g + np.where(s < 8, 0, np.where(s < 16, 1, np.where(s < 20, 0, 1)))
    n = np.where(s < 8, s, np.where(s < 16, s - 8, np.where(s < 20, s - 8, s - 12)))
    src = np.where(j < 120, CH * n + c, j)
    return (src[:, None] == np.arange(128)[None, :]).astype(np.float32)


def back_matrix():
    out = np.zeros((96, 256), np.float32)
    for g in range(5):
        for s in range(16):
            if s < 12:
                out[16 * g + s, CH * s + 2 * g] = 1
            if s < 8 or s >= 12:
                n = s if s < 8 else s - 4
                out[16 * g + s, 128 + CH * n + 2 * g + 1] = 1
    for s in range(8):
        out[80 + s, 120 + s] = 1
    return out


def last_matrix():
    out = np.zeros((256, 128), np.float32)
    for o in range(ROWS):
        for t in range(4):
            out[16 * o + 8 + t, 8 * o + t] = 1
    return out


def sines():
    i = np.arange(192, dtype=np.float64) - R
    return np.sin(np.pi * (i + 0.5) / 180.0).astype(np.float32)[None]


def build_weights(sup_ref, sin_ref, start, t_ref):
    lane = iota((16, 128), 1)
    rlane = lane // 16
    s = lane % 16
    n_in = jnp.where(s < 12, s, s - 4)
    sub = iota((16, 128), 0)
    n_out = jnp.where(sub < 12, sub, sub - 4)
    diff = (n_in - n_out).astype(F32)

    def one(o, carry):
        local = o % 4
        group = o // 4
        row = jnp.minimum(start + o, 179)
        d = rlane - local
        width = jnp.ones((16, 128), F32)
        sine = jnp.zeros((16, 128), F32)
        for j in range(2 * R + 1):
            width = jnp.where(d == j, sup_ref[j, row].astype(F32), width)
            sine = jnp.where(d == j, sin_ref[0, row + j], sine)
        ok = (d >= 0) & (d <= 2 * R)
        scale = jnp.where(ok, sine / jnp.sqrt((2.0 * R + 1.0) * (2.0 * width + 1.0)), 0.0)
        lat = (d - R).astype(F32) / (R + 1.0)
        lat2 = lat * lat
        base = pl.multiple_of(local * 64, 64)
        for step in range(9):
            m = diff + float(12 * (step - 4))
            lon = m / (width + 1.0)
            radius = jnp.sqrt(lat2 + lon * lon) * (K - 1.0)
            w = jnp.where(jnp.abs(m) <= width, scale, 0.0)
            for k in range(K):
                hat = jnp.maximum(0.0, 1.0 - jnp.abs(radius - float(k)))
                t_ref[group, pl.ds(base + 16 * k, 16), pl.ds(128 * step, 128)] = (hat * w).astype(BF)
        return carry

    lax.fori_loop(0, 16, one, 0)


def build_filter(filt_ref, me, w_ref):
    lane = iota((C, 768), 1)
    chan = lane // 64
    want = jnp.where(chan < CH, me * CH + chan, C - 1)
    pick = jnp.where(iota((C, 768), 0) == want, 1.0, 0.0).astype(BF)
    w_ref[...] = jnp.dot(filt_ref[...], pick, preferred_element_type=F32)


NT = (((1,), (1,)), ((), ()))
TN = (((0,), (0,)), ((), ()))


def rows_of(x_ref, r):
    return x_ref[pl.ds(r, 64, stride=16), :].astype(BF)


def twice(x):
    return jnp.concatenate([x, x], axis=0)


def turn_rows(order_ref, parts, first, last, rows, d_ref, e_ref):
    eye = (iota((128, 128), 0) == iota((128, 128), 1)).astype(F32).astype(BF)
    order = order_ref[...]
    ex = lax.dot_general(eye, twice(last), NT, preferred_element_type=F32)
    for i, r in enumerate(rows):
        d_ref[first + i] = lax.dot_general(order, twice(parts[i]), NT, preferred_element_type=F32)
        e_ref[first + i] = ex[8 * r : 8 * r + 8]


def spread_rows(start, stop, d_ref, e_ref, f_ref):
    lane8 = iota((8, 128), 1)
    sub8 = iota((8, 128), 0)
    left = lane8 < 64
    both = (sub8 < 4) == left
    corner = (sub8 < 4) & left

    def one(r, carry):
        at = pl.multiple_of(16 * r, 16)
        for step in range(9):
            shift = (4 - step) % 128
            turned = d_ref[r]
            ex = e_ref[r]
            if shift:
                turned = pltpu.roll(turned, shift, 1)
                ex = pltpu.roll(ex, shift, 1)
            for g in range(6):
                if g < 5:
                    top = jnp.where(left, turned[24 * g : 24 * g + 8], turned[24 * g + 8 : 24 * g + 16])
                    low = jnp.where(both, turned[24 * g + 16 : 24 * g + 24], 0.0)
                else:
                    top = jnp.where(left, turned[120:128], 0.0)
                    low = jnp.where(corner, ex, 0.0)
                f_ref[step, pl.ds(at, 16), pl.ds(128 * g, 128)] = jnp.concatenate([top, low], axis=0).astype(BF)
        return carry

    lax.fori_loop(start, stop, one, 0)


def convolve(t_ref, f_ref, w_ref, back_ref, final_ref, acc_ref, x_ref, z_ref, out_ref):
    def group(g, carry):
        at = pl.multiple_of(64 * g, 64)
        for j in range(3):
            rhs = jnp.concatenate([f_ref[step, pl.ds(at, 128), pl.ds(256 * j, 256)] for step in range(9)], axis=0)
            acc_ref[:, pl.ds(256 * j, 256)] = jnp.dot(t_ref[g], rhs, preferred_element_type=F32)
        for o in range(4):
            conv = jnp.zeros((16, 768), F32)
            for k in range(K):
                conv = conv + acc_ref[pl.ds(64 * o + 16 * k, 16), :] * w_ref[pl.ds(k, 1), :]
            centre = f_ref[4, pl.ds(at + 16 * (o + R), 16), :].astype(F32)
            comb = (centre + conv).astype(BF)
            stack = jnp.concatenate([comb[:, 128 * i : 128 * i + 128] for i in range(6)], axis=0)
            moved = lax.dot_general(stack, back_ref[...], TN, preferred_element_type=F32)
            x_ref[pl.ds(4 * g + o, 64, stride=16), :] = moved[:64, :128] + moved[64:, 128:]
            z_ref[pl.ds(at + 16 * o, 16), :] = comb[:, 640:]
        return carry

    lax.fori_loop(0, 4, group, 0)
    last = lax.dot_general(z_ref[...], final_ref[...], TN, preferred_element_type=F32)
    x_ref[pl.ds(15, 64, stride=16), :] = last[:64]
    out_ref[...] = x_ref[...].reshape(64, 16, 128).astype(BF)


def mlp(c_ref, up_ref, down_ref, out_ref):
    lane = iota((192, 768), 1)
    values = c_ref[...]
    mean = jnp.sum(values, axis=1, keepdims=True) * (1.0 / C)
    centered = jnp.where(lane < C, values - mean, 0.0)
    spread = jnp.sum(centered * centered, axis=1, keepdims=True) * (1.0 / C)
    normed = (centered * lax.rsqrt(spread + 1e-05)).astype(BF)[:, :C]
    raised = jnp.dot(normed, up_ref[...], preferred_element_type=F32)
    hidden = (0.5 * raised * (1.0 + lax.erf(raised * math.sqrt(0.5)))).astype(BF)
    lowered = lax.dot_general(hidden, down_ref[...], NT, preferred_element_type=F32)
    result = (values[:, :C] + lowered).astype(BF)
    for n in range(NB):
        out_ref[n] = result[16 * n : 16 * n + ROWS]


def hail(me, lat, lats, barrier):
    def one(i, carry):
        pl.semaphore_signal(barrier, inc=1, device_id={"lon": lax.rem(me + i, OWN)}, device_id_type=MESH)
        return carry

    lax.fori_loop(1, OWN, one, 0)

    @pl.when(lat > 0)
    def _():
        pl.semaphore_signal(barrier, inc=1, device_id={"lat": lat - 1}, device_id_type=MESH)

    @pl.when(lat < lats - 1)
    def _():
        pl.semaphore_signal(barrier, inc=1, device_id={"lat": lat + 1}, device_id_type=MESH)


def send_all(me, src, dst, send_sem, recv_sem):
    across, along, up = me // 16, me // 8 % 2, me % 8

    def send(i, side):
        p = lax.rem(across + i // 8, 4) * 16 + side * 8 + lax.rem(up + i % 8, 8)
        pltpu.make_async_remote_copy(
            src.at[p], dst.at[me], send_sem, recv_sem, device_id={"lon": p}, device_id_type=MESH
        ).start()

    def far(i, carry):
        send(i, 1 - along)
        return carry

    def near(i, carry):
        send(i, along)
        return carry

    lax.fori_loop(0, 32, far, 0)
    lax.fori_loop(1, 32, near, 0)


def all_sent(me, src, dst, send_sem, recv_sem):
    return pltpu.make_async_remote_copy(
        src.at[pl.ds(0, OWN - 1)], dst.at[pl.ds(0, OWN - 1)], send_sem, recv_sem,
        device_id={"lon": lax.rem(me + 1, OWN)}, device_id_type=MESH,
    )


def kernel(lats, pts_hbm, sup_ref, sin_ref, filt_ref, order_ref, back_ref, final_ref, wup_hbm, wdown_hbm, out_ref,
           pts, wup, wdown, roll_ref, msg, own, halo_out, halo_in, t_ref, w_ref, x_ref, d_ref, e_ref, f_ref, acc_ref,
           z_ref, back, pieces, turn_ref, c_ref, load_sem, send_sem, recv_sem, halo_send, halo_recv):
    me = lax.axis_index("lon")
    lat = lax.axis_index("lat")
    barrier = pltpu.get_barrier_semaphore()
    fetch = pltpu.make_async_copy(pts_hbm, pts, load_sem.at[0])
    fetch.start()
    hail(me, lat, lats, barrier)
    fetch_up = pltpu.make_async_copy(wup_hbm, wup, load_sem.at[1])
    fetch_down = pltpu.make_async_copy(wdown_hbm, wdown, load_sem.at[2])
    fetch_up.start()
    fetch_down.start()
    fetch.wait()
    pack(pts, msg, roll_ref)
    pl.semaphore_wait(barrier, OWN - 1 + (lat > 0).astype(jnp.int32) + (lat < lats - 1).astype(jnp.int32))
    send_all(me, msg, own, send_sem.at[0], recv_sem.at[0])
    own[me] = msg[me]
    build_weights(sup_ref, sin_ref, lat * ROWS, t_ref)
    build_filter(filt_ref, me, w_ref)
    for step in range(9):
        f_ref[step, pl.ds(304, 16), :] = jnp.zeros((16, 768), BF)
    first = all_sent(me, msg, own, send_sem.at[0], recv_sem.at[0])
    first.wait_recv()

    def halo(to, i):
        return pltpu.make_async_remote_copy(
            halo_out.at[i], halo_in.at[i], halo_send.at[i], halo_recv.at[i], device_id={"lat": to}, device_id_type=MESH
        )

    x_ref[...] = own[...].reshape(1024, 128).astype(F32)
    last = rows_of(x_ref, 15)
    for i, rows in enumerate(((0, 1), (13, 14))):
        for j, r in enumerate(rows):
            halo_out[i, j] = rows_of(x_ref, r)
        halo_out[i, 2] = last

    @pl.when(lat > 0)
    def _():
        halo(lat - 1, 0).start()

    @pl.when(lat < lats - 1)
    def _():
        halo(lat + 1, 1).start()

    turn_rows(order_ref, [rows_of(x_ref, r) for r in range(ROWS)], R, last, range(ROWS), d_ref, e_ref)
    spread_rows(R, ROWS + R, d_ref, e_ref, f_ref)

    @pl.when(lat > 0)
    def _():
        halo(lat - 1, 0).wait_send()
        halo(lat - 1, 1).wait_recv()

    @pl.when(lat == 0)
    def _():
        halo_in[1] = jnp.zeros((3, OWN, 128), BF)

    @pl.when(lat < lats - 1)
    def _():
        halo(lat + 1, 1).wait_send()
        halo(lat + 1, 0).wait_recv()

    @pl.when(lat == lats - 1)
    def _():
        halo_in[0] = jnp.zeros((3, OWN, 128), BF)

    turn_rows(order_ref, [halo_in[1, 0], halo_in[1, 1]], 0, halo_in[1, 2], (13, 14), d_ref, e_ref)
    turn_rows(order_ref, [halo_in[0, 0], halo_in[0, 1]], ROWS + R, halo_in[0, 2], (0, 1), d_ref, e_ref)
    spread_rows(0, R, d_ref, e_ref, f_ref)
    spread_rows(ROWS + R, ROWS + 2 * R, d_ref, e_ref, f_ref)
    convolve(t_ref, f_ref, w_ref, back_ref, final_ref, acc_ref, x_ref, z_ref, back)
    send_all(me, back, pieces, send_sem.at[1], recv_sem.at[1])
    pieces[me] = back[me]
    fetch_up.wait()
    fetch_down.wait()
    first.wait_send()
    second = all_sent(me, back, pieces, send_sem.at[1], recv_sem.at[1])
    second.wait_recv()
    unpack(pieces, c_ref, turn_ref)
    mlp(c_ref, wup, wdown, out_ref)
    second.wait_send()


VM = pl.BlockSpec(memory_space=pltpu.VMEM)
SM = pl.BlockSpec(memory_space=pltpu.SMEM)
ANY = pl.BlockSpec(memory_space=pl.ANY)


def on_device(lats, fields, support, filter_weight, w_up, w_down):
    points = jnp.transpose(fields, (2, 0, 1))
    dma = pltpu.SemaphoreType.DMA
    result = pl.pallas_call(
        functools.partial(kernel, lats), out_shape=jax.ShapeDtypeStruct((NB, ROWS, C), BF),
        in_specs=[ANY, SM, SM, VM, VM, VM, VM, ANY, ANY], out_specs=VM,
        scratch_shapes=[
            pltpu.VMEM((NB, ROWS, C), BF), pltpu.VMEM(w_up.shape, BF), pltpu.VMEM(w_up.shape, BF),
            pltpu.VMEM((NB, 16, 768), F32), pltpu.VMEM((OWN, 16, 128), BF), pltpu.VMEM((OWN, 16, 128), BF),
            pltpu.VMEM((2, 3, OWN, 128), BF), pltpu.VMEM((2, 3, OWN, 128), BF),
            pltpu.VMEM((4, 256, 1152), BF), pltpu.VMEM((K, 768), F32), pltpu.VMEM((1024, 128), F32),
            pltpu.VMEM((ROWS + 2 * R, 128, 128), F32), pltpu.VMEM((ROWS + 2 * R, 8, 128), F32),
            pltpu.VMEM((9, 320, 768), BF), pltpu.VMEM((256, 768), F32), pltpu.VMEM((256, 128), BF),
            pltpu.VMEM((OWN, 16, 128), BF), pltpu.VMEM((OWN, 16, 128), BF),
            pltpu.VMEM((OWN, 16, 128), F32), pltpu.VMEM((192, 768), F32),
            dma((3,)), dma((2,)), dma((2,)), dma((2,)), dma((2,)),
        ],
        compiler_params=pltpu.CompilerParams(vmem_limit_bytes=60 << 20, collective_id=0, has_side_effects=True),
        name="block",
    )(points, support.T, jnp.asarray(sines()), filter_weight.T, jnp.asarray(order_matrix(), BF),
      jnp.asarray(back_matrix(), BF), jnp.asarray(last_matrix(), BF), w_up, w_down.T)
    return jnp.transpose(result, (1, 2, 0))


def solution(mesh):
    in_specs = (P("lat", None, "lon"), P(), P(), P(), P())
    out_specs = P("lat", None, "lon")
    return jax.shard_map(
        functools.partial(on_device, mesh.shape["lat"]), mesh=mesh, in_specs=in_specs, out_specs=out_specs,
        check_vma=False,
    )
```

```python
import functools
import math

import jax
import jax.numpy as jnp
import numpy as np
from jax import lax
from jax.experimental import pallas as pl
from jax.experimental.pallas import tpu as pltpu
from jax.sharding import PartitionSpec as P

MESH = pl.DeviceIdType.MESH
NB = 12
ROWS = 15
C = 641
CH = 10
OWN = 64
K = 4
R = 2
F32 = jnp.float32
BF = jnp.bfloat16


def iota(shape, dim):
    return lax.broadcasted_iota(jnp.int32, shape, dim)


HALF = 5


def prepare(f_ref, roll_ref, last_ref):
    lane = iota((16, 128), 1)
    sub = iota((16, 128), 0)
    lane8 = iota((8, 128), 1)
    spread = jnp.zeros((16, 128), F32)
    extras = [jnp.zeros((16, 128), F32), jnp.zeros((16, 128), F32)]
    for n in range(NB):
        x = f_ref[n].astype(F32)
        x = jnp.concatenate([x, jnp.zeros((ROWS, 768 - C), F32)], axis=1)
        x = jnp.concatenate([x, jnp.zeros((1, 768), F32)], axis=0)
        roll_ref[n] = pltpu.roll(x, HALF * n, 1) if n else x
        col = jnp.broadcast_to(x[:, 640:641], (16, 128))
        if n < 8:
            extras[n // 4] = jnp.where(lane % 64 == 60 + n % 4, col, extras[n // 4])
        else:
            spread = jnp.where(lane == 64 + 4 * sub + (n - 8), col, spread)
    row = jnp.sum(jnp.where(sub < ROWS, spread, 0.0), axis=0, keepdims=True)
    for h in range(2):
        last_ref[h] = jnp.where(lane8 < 64, extras[h][:8], extras[h][8:])
    last_ref[2] = jnp.broadcast_to(row, (8, 128))


def pack(h, roll_ref, last_ref, o_ref):
    lane = iota((8, 128), 1)
    sub = iota((8, 128), 0)
    for p in range(OWN):
        begin = CH * p + HALF * h
        cut = begin % 128
        here = (lane - cut) & 127
        acc = [None, None]
        for n in range(NB):
            lo = begin + HALF * n
            first, final = lo // 128, (lo + HALF - 1) // 128
            for i in range(2):
                x = roll_ref[n, pl.ds(8 * i, 8), pl.ds(first * 128, 128)]
                if first != final:
                    x = jnp.where(lane >= 64, x, roll_ref[n, pl.ds(8 * i, 8), pl.ds(final * 128, 128)])
                acc[i] = x if n == 0 else jnp.where(here >= HALF * n, x, acc[i])
        low = pltpu.roll(acc[0], 128 - cut, 1) if cut else acc[0]
        high = pltpu.roll(acc[1], (192 - cut) % 128, 1) if cut != 64 else acc[1]
        x = jnp.where(lane < 64, low, high)
        x = jnp.where((lane & 63) >= 60, last_ref[h], x)
        if h:
            x = jnp.where((sub == 7) & (lane >= 64) & (lane < 124), last_ref[2], x)
        o_ref[h, p] = x.astype(BF)


def turn_pieces(h, m_ref, turn_ref):
    for q in range(OWN):
        x = m_ref[h, q].astype(F32)
        cut = (CH * q + HALF * h) % 128
        turn_ref[2 * q + h, pl.ds(0, 8), :] = pltpu.roll(x, cut, 1) if cut else x
        turn_ref[2 * q + h, pl.ds(8, 8), :] = pltpu.roll(x, (cut + 64) % 128, 1) if cut != 64 else x


def unpack(turn_ref, last, c_ref):
    lane = iota((16, 128), 1)
    for n in range(NB):
        tiles = []
        for t in range(6):
            acc = jnp.zeros((16, 128), F32)
            for i in range(2 * OWN):
                a = HALF * (i + n) - t * 128
                if -HALF < a < 128:
                    acc = turn_ref[i] if a <= 0 else jnp.where(lane >= a, turn_ref[i], acc)
            tiles.append(acc)
        full = jnp.concatenate(tiles, axis=1)
        if n:
            full = pltpu.roll(full, 768 - HALF * n, 1)
        c_ref[pl.ds(16 * n, 16), pl.ds(0, 640)] = full[:, :640]
        c_ref[pl.ds(16 * n, 16), pl.ds(640, 128)] = jnp.where(lane == 0, last[:, n : n + 1], 0.0)


def order_matrix():
    out = np.zeros((2, 2, 64, 128), np.float32)
    for h in range(2):
        for half in range(2):
            base = 64 * half
            for g in range(2):
                for n in range(NB):
                    for c in range(2):
                        j = 24 * g + (8 * c + n if n < 8 else 16 + 4 * c + n - 8)
                        out[h, half, j, base + HALF * n + 2 * g + c] = 1
            for n in range(NB):
                j = 48 + n if n < 8 or h else 48 + n + 4
                out[h, half, j, base + HALF * n + 4] = 1
            for t in range(4):
                out[h, half, 60 + t if h else 56 + t, base + 60 + t] = 1
    return out


def row_matrix():
    out = np.zeros((128, 128), np.float32)
    for r in range(ROWS):
        for t in range(4):
            out[8 * r + t, 64 + 4 * r + t] = 1
    return out


def back_matrix():
    out = np.zeros((2, 2, 48, 384), np.float32)
    for h in range(2):
        for half in range(2):
            base = 64 * half
            for n in range(NB):
                for g in range(2):
                    out[h, half, 16 * g + n, base + HALF * n + 2 * g] = 1
                    out[h, half, 16 * g + (n if n < 8 else n + 4), 128 + base + HALF * n + 2 * g + 1] = 1
                out[h, half, 32 + (n if n < 8 or h else n + 4), base + HALF * n + 4] = 1
                out[h, half, 32 + n, 256 + n] = 1
    return out


def sines():
    i = np.arange(192, dtype=np.float64) - R
    return np.sin(np.pi * (i + 0.5) / 180.0).astype(np.float32)[None]


def build_weights(sup_ref, sin_ref, start, t_ref):
    lane = iota((16, 128), 1)
    rlane = lane // 16
    s = lane % 16
    n_in = jnp.where(s < 12, s, s - 4)
    sub = iota((16, 128), 0)
    n_out = jnp.where(sub < 12, sub, sub - 4)
    diff = (n_in - n_out).astype(F32)

    def one(o, carry):
        local = o % 4
        group = o // 4
        row = jnp.minimum(start + o, 179)
        d = rlane - local
        width = jnp.ones((16, 128), F32)
        sine = jnp.zeros((16, 128), F32)
        for j in range(2 * R + 1):
            width = jnp.where(d == j, sup_ref[j, row].astype(F32), width)
            sine = jnp.where(d == j, sin_ref[0, row + j], sine)
        ok = (d >= 0) & (d <= 2 * R)
        scale = jnp.where(ok, sine / jnp.sqrt((2.0 * R + 1.0) * (2.0 * width + 1.0)), 0.0)
        lat = (d - R).astype(F32) / (R + 1.0)
        lat2 = lat * lat
        base = pl.multiple_of(local * 64, 64)
        for step in range(9):
            m = diff + float(12 * (step - 4))
            lon = m / (width + 1.0)
            radius = jnp.sqrt(lat2 + lon * lon) * (K - 1.0)
            w = jnp.where(jnp.abs(m) <= width, scale, 0.0)
            for k in range(K):
                hat = jnp.maximum(0.0, 1.0 - jnp.abs(radius - float(k)))
                t_ref[group, pl.ds(base + 16 * k, 16), pl.ds(128 * step, 128)] = (hat * w).astype(BF)
        return carry

    lax.fori_loop(0, 16, one, 0)


def build_filter(filt_ref, me, w_ref):
    lane = iota((C, 768), 1)
    slot = lane // 64 % 6
    chan = me * CH + HALF * (lane // 384) + slot
    want = jnp.where(slot == 5, C - 1, chan)
    pick = jnp.where(iota((C, 768), 0) == want, 1.0, 0.0).astype(BF)
    w_ref[...] = jnp.dot(filt_ref[...], pick, preferred_element_type=F32)


NT = (((1,), (1,)), ((), ()))
TN = (((0,), (0,)), ((), ()))


def rows_of(x_ref, r):
    return x_ref[pl.ds(r % 8, 64, stride=8), :].astype(BF)


def twice(x):
    return jnp.concatenate([x, x], axis=0)


def turn_rows(h, order_ref, row_ref, parts, last, first, rows, d_ref, e_ref, z_ref):
    if h:
        ex = lax.dot_general(row_ref[...], twice(last), NT, preferred_element_type=F32)
    for i, r in enumerate(rows):
        turned = lax.dot_general(order_ref[h, r // 8], twice(parts[i]), NT, preferred_element_type=F32)
        d_ref[first + i] = turned
        if h:
            e_ref[first + i] = ex[8 * r : 8 * r + 8]
        else:
            z_ref[first + i] = turned[56:64]


def spread_rows(h, start, stop, d_ref, e_ref, z_ref, f_ref):
    lane8 = iota((8, 128), 1)
    sub8 = iota((8, 128), 0)
    left = lane8 < 64
    upper = sub8 < 4
    both = upper == left

    def one(r, carry):
        at = pl.multiple_of(16 * r, 16)
        for step in range(9):
            shift = (4 - step) % 128

            def roll(x):
                return pltpu.roll(x, shift, 1) if shift else x

            turned = roll(d_ref[r])
            for g in range(3):
                if g < 2:
                    top = jnp.where(left, turned[24 * g : 24 * g + 8], turned[24 * g + 8 : 24 * g + 16])
                    low = jnp.where(both, turned[24 * g + 16 : 24 * g + 24], 0.0)
                elif h:
                    tail = turned[56:64]
                    top = jnp.where(left, turned[48:56], jnp.where(upper, roll(z_ref[r]), tail))
                    low = jnp.where(upper, jnp.where(left, tail, roll(e_ref[r])), 0.0)
                else:
                    top = jnp.where(left, turned[48:56], 0.0)
                    low = jnp.where(left & (sub8 >= 4), turned[56:64], 0.0)
                f_ref[step, pl.ds(at, 16), pl.ds(128 * g, 128)] = jnp.concatenate([top, low], axis=0).astype(BF)
        return carry

    lax.fori_loop(start, stop, one, 0)


def convolve(h, groups, t_ref, f_ref, w_ref, back_ref, acc_ref, x_ref, ex_ref):
    for g in groups:
        at = 64 * g
        rhs = jnp.concatenate([f_ref[step, pl.ds(at, 128), :] for step in range(9)], axis=0)
        acc_ref[...] = jnp.dot(t_ref[g], rhs, preferred_element_type=F32)
        for o in range(4):
            conv = jnp.zeros((16, 384), F32)
            for k in range(K):
                conv = conv + acc_ref[pl.ds(64 * o + 16 * k, 16), :] * w_ref[pl.ds(k, 1), pl.ds(384 * h, 384)]
            centre = f_ref[4, pl.ds(at + 16 * (o + R), 16), :].astype(F32)
            comb = (centre + conv).astype(BF)
            stack = jnp.concatenate([comb[:, 128 * i : 128 * i + 128] for i in range(3)], axis=0)
            moved = lax.dot_general(stack, back_ref[h, g // 2], TN, preferred_element_type=F32)
            value = moved[:64, :128] + moved[64:, 128:256]
            row = (4 * g + o) % 8
            if g in (0, 3):
                value = value + x_ref[pl.ds(row, 64, stride=8), :]
            x_ref[pl.ds(row, 64, stride=8), :] = value
            if h:
                ex_ref[4 * g + o] = moved[64:, 256:]


def mlp(c_ref, up_ref, down_ref, out_ref):
    lane = iota((192, 768), 1)
    values = c_ref[...]
    mean = jnp.sum(values, axis=1, keepdims=True) * (1.0 / C)
    centered = jnp.where(lane < C, values - mean, 0.0)
    spread = jnp.sum(centered * centered, axis=1, keepdims=True) * (1.0 / C)
    normed = (centered * lax.rsqrt(spread + 1e-05)).astype(BF)[:, :C]
    raised = jnp.dot(normed, up_ref[...], preferred_element_type=F32)
    hidden = (0.5 * raised * (1.0 + lax.erf(raised * math.sqrt(0.5)))).astype(BF)
    lowered = lax.dot_general(hidden, down_ref[...], NT, preferred_element_type=F32)
    result = (values[:, :C] + lowered).astype(BF)
    for n in range(NB):
        out_ref[n] = result[16 * n : 16 * n + ROWS]


def hail(me, lat, lats, barrier):
    def one(i, carry):
        pl.semaphore_signal(barrier, inc=1, device_id={"lon": lax.rem(me + i, OWN)}, device_id_type=MESH)
        return carry

    lax.fori_loop(1, OWN, one, 0)

    @pl.when(lat > 0)
    def _():
        pl.semaphore_signal(barrier, inc=1, device_id={"lat": lat - 1}, device_id_type=MESH)

    @pl.when(lat < lats - 1)
    def _():
        pl.semaphore_signal(barrier, inc=1, device_id={"lat": lat + 1}, device_id_type=MESH)


def send_all(me, src, dst, send_sem, recv_sem):
    across, along, up = me // 16, me // 8 % 2, me % 8

    def send(i, side):
        p = lax.rem(across + i // 8, 4) * 16 + side * 8 + lax.rem(up + i % 8, 8)
        pltpu.make_async_remote_copy(
            src.at[p], dst.at[me], send_sem, recv_sem, device_id={"lon": p}, device_id_type=MESH
        ).start()

    def far(i, carry):
        send(i, 1 - along)
        return carry

    def near(i, carry):
        send(i, along)
        return carry

    lax.fori_loop(0, 32, far, 0)
    lax.fori_loop(1, 32, near, 0)


def all_sent(me, src, dst, send_sem, recv_sem):
    return pltpu.make_async_remote_copy(
        src.at[pl.ds(0, OWN - 1)], dst.at[pl.ds(0, OWN - 1)], send_sem, recv_sem,
        device_id={"lon": lax.rem(me + 1, OWN)}, device_id_type=MESH,
    )


def kernel(lats, pts_hbm, sup_ref, sin_ref, filt_ref, order_ref, row_ref, back_ref, wup_hbm, wdown_hbm, out_ref,
           pts, wup, wdown, roll_ref, last_ref, msg, own, halo_out, halo_in, t_ref, w_ref, x_ref, d_ref, e_ref, z_ref,
           f_ref, acc_ref, ex_ref, back, pieces, turn_ref, c_ref, load_sem, send_sem, recv_sem, halo_send, halo_recv):
    me = lax.axis_index("lon")
    lat = lax.axis_index("lat")
    barrier = pltpu.get_barrier_semaphore()
    fetch = pltpu.make_async_copy(pts_hbm, pts, load_sem.at[0])
    fetch.start()
    hail(me, lat, lats, barrier)
    fetch_up = pltpu.make_async_copy(wup_hbm, wup, load_sem.at[1])
    fetch_down = pltpu.make_async_copy(wdown_hbm, wdown, load_sem.at[2])
    fetch_up.start()
    fetch_down.start()
    fetch.wait()
    prepare(pts, roll_ref, last_ref)
    pack(0, roll_ref, last_ref, msg)
    pl.semaphore_wait(barrier, OWN - 1 + (lat > 0).astype(jnp.int32) + (lat < lats - 1).astype(jnp.int32))
    send_all(me, msg.at[0], own.at[0], send_sem.at[0], recv_sem.at[0])
    pack(1, roll_ref, last_ref, msg)
    send_all(me, msg.at[1], own.at[1], send_sem.at[1], recv_sem.at[1])
    for h in range(2):
        own[h, me] = msg[h, me]
    build_weights(sup_ref, sin_ref, lat * ROWS, t_ref)
    build_filter(filt_ref, me, w_ref)
    for step in range(9):
        f_ref[step, pl.ds(304, 16), :] = jnp.zeros((16, 384), BF)

    def halo(h, to, i):
        return pltpu.make_async_remote_copy(
            halo_out.at[h, i], halo_in.at[h, i], halo_send.at[h, i], halo_recv.at[h, i],
            device_id={"lat": to}, device_id_type=MESH,
        )

    for h in range(2):
        all_sent(me, msg.at[h], own.at[h], send_sem.at[h], recv_sem.at[h]).wait_recv()
        x_ref[...] = own[h].reshape(512, 128).astype(F32)
        for i, rows in enumerate(((0, 1), (13, 14))):
            for j, r in enumerate(rows):
                halo_out[h, i, j] = rows_of(x_ref, r)
            halo_out[h, i, 2] = rows_of(x_ref, 15)

        @pl.when(lat > 0)
        def _():
            halo(h, lat - 1, 0).start()

        @pl.when(lat < lats - 1)
        def _():
            halo(h, lat + 1, 1).start()

        turn_rows(h, order_ref, row_ref, [rows_of(x_ref, r) for r in range(ROWS)], rows_of(x_ref, 15), R, range(ROWS),
                  d_ref, e_ref, z_ref)
        spread_rows(h, R, ROWS + R, d_ref, e_ref, z_ref, f_ref)
        convolve(h, (1, 2), t_ref, f_ref, w_ref, back_ref, acc_ref, x_ref, ex_ref)

        @pl.when(lat > 0)
        def _():
            halo(h, lat - 1, 1).wait_recv()

        @pl.when(lat == 0)
        def _():
            halo_in[h, 1] = jnp.zeros((3, OWN, 128), BF)

        @pl.when(lat < lats - 1)
        def _():
            halo(h, lat + 1, 0).wait_recv()

        @pl.when(lat == lats - 1)
        def _():
            halo_in[h, 0] = jnp.zeros((3, OWN, 128), BF)

        turn_rows(h, order_ref, row_ref, [halo_in[h, 1, 0], halo_in[h, 1, 1]], halo_in[h, 1, 2], 0, (13, 14),
                  d_ref, e_ref, z_ref)
        turn_rows(h, order_ref, row_ref, [halo_in[h, 0, 0], halo_in[h, 0, 1]], halo_in[h, 0, 2], ROWS + R, (0, 1),
                  d_ref, e_ref, z_ref)
        spread_rows(h, 0, R, d_ref, e_ref, z_ref, f_ref)
        spread_rows(h, ROWS + R, ROWS + 2 * R, d_ref, e_ref, z_ref, f_ref)
        convolve(h, (0, 3), t_ref, f_ref, w_ref, back_ref, acc_ref, x_ref, ex_ref)
        back[h] = x_ref[...].reshape(64, 8, 128).astype(BF)
        send_all(me, back.at[h], pieces.at[h], send_sem.at[2 + h], recv_sem.at[2 + h])
        pieces[h, me] = back[h, me]
    fetch_up.wait()
    fetch_down.wait()
    for h in range(2):
        all_sent(me, msg.at[h], own.at[h], send_sem.at[h], recv_sem.at[h]).wait_send()

        @pl.when(lat > 0)
        def _():
            halo(h, lat - 1, 0).wait_send()

        @pl.when(lat < lats - 1)
        def _():
            halo(h, lat + 1, 1).wait_send()

    last = jnp.concatenate([ex_ref[o, pl.ds(me, 1), :] for o in range(16)], axis=0)
    for h in range(2):
        all_sent(me, back.at[h], pieces.at[h], send_sem.at[2 + h], recv_sem.at[2 + h]).wait_recv()
        turn_pieces(h, pieces, turn_ref)
    unpack(turn_ref, last, c_ref)
    mlp(c_ref, wup, wdown, out_ref)
    for h in range(2):
        all_sent(me, back.at[h], pieces.at[h], send_sem.at[2 + h], recv_sem.at[2 + h]).wait_send()


VM = pl.BlockSpec(memory_space=pltpu.VMEM)
SM = pl.BlockSpec(memory_space=pltpu.SMEM)
ANY = pl.BlockSpec(memory_space=pl.ANY)


def on_device(lats, fields, support, filter_weight, w_up, w_down):
    points = jnp.transpose(fields, (2, 0, 1))
    dma = pltpu.SemaphoreType.DMA
    result = pl.pallas_call(
        functools.partial(kernel, lats), out_shape=jax.ShapeDtypeStruct((NB, ROWS, C), BF),
        in_specs=[ANY, SM, SM, VM, VM, VM, VM, ANY, ANY], out_specs=VM,
        scratch_shapes=[
            pltpu.VMEM((NB, ROWS, C), BF), pltpu.VMEM(w_up.shape, BF), pltpu.VMEM(w_up.shape, BF),
            pltpu.VMEM((NB, 16, 768), F32), pltpu.VMEM((3, 8, 128), F32),
            pltpu.VMEM((2, OWN, 8, 128), BF), pltpu.VMEM((2, OWN, 8, 128), BF),
            pltpu.VMEM((2, 2, 3, OWN, 128), BF), pltpu.VMEM((2, 2, 3, OWN, 128), BF),
            pltpu.VMEM((4, 256, 1152), BF), pltpu.VMEM((K, 768), F32), pltpu.VMEM((512, 128), F32),
            pltpu.VMEM((ROWS + 2 * R, 64, 128), F32), pltpu.VMEM((ROWS + 2 * R, 8, 128), F32),
            pltpu.VMEM((ROWS + 2 * R, 8, 128), F32),
            pltpu.VMEM((9, 320, 384), BF), pltpu.VMEM((256, 384), F32), pltpu.VMEM((16, OWN, 128), F32),
            pltpu.VMEM((2, OWN, 8, 128), BF), pltpu.VMEM((2, OWN, 8, 128), BF),
            pltpu.VMEM((2 * OWN, 16, 128), F32), pltpu.VMEM((192, 768), F32),
            dma((3,)), dma((4,)), dma((4,)), dma((2, 2)), dma((2, 2)),
        ],
        compiler_params=pltpu.CompilerParams(vmem_limit_bytes=60 << 20, collective_id=0, has_side_effects=True),
        name="block",
    )(points, support.T, jnp.asarray(sines()), filter_weight.T, jnp.asarray(order_matrix(), BF),
      jnp.asarray(row_matrix(), BF), jnp.asarray(back_matrix(), BF), w_up, w_down.T)
    return jnp.transpose(result, (1, 2, 0))


def solution(mesh):
    in_specs = (P("lat", None, "lon"), P(), P(), P(), P())
    out_specs = P("lat", None, "lon")
    return jax.shard_map(
        functools.partial(on_device, mesh.shape["lat"]), mesh=mesh, in_specs=in_specs, out_specs=out_specs,
        check_vma=False,
    )
```

```python
import functools
import math

import jax
import jax.numpy as jnp
import numpy as np
from jax import lax
from jax.experimental import pallas as pl
from jax.experimental.pallas import tpu as pltpu
from jax.sharding import PartitionSpec as P

MESH = pl.DeviceIdType.MESH
NB = 12
ROWS = 15
C = 641
CH = 10
OWN = 64
K = 4
R = 2
F32 = jnp.float32
BF = jnp.bfloat16


def iota(shape, dim):
    return lax.broadcasted_iota(jnp.int32, shape, dim)


HALF = 5


def prepare(f_ref, roll_ref, last_ref):
    lane = iota((16, 128), 1)
    sub = iota((16, 128), 0)
    lane8 = iota((8, 128), 1)
    spread = jnp.zeros((16, 128), F32)
    extras = [jnp.zeros((16, 128), F32), jnp.zeros((16, 128), F32)]
    for n in range(NB):
        x = f_ref[n].astype(F32)
        x = jnp.concatenate([x, jnp.zeros((ROWS, 768 - C), F32)], axis=1)
        x = jnp.concatenate([x, jnp.zeros((1, 768), F32)], axis=0)
        roll_ref[n] = pltpu.roll(x, HALF * n, 1) if n else x
        col = jnp.broadcast_to(x[:, 640:641], (16, 128))
        if n < 8:
            extras[n // 4] = jnp.where(lane % 64 == 60 + n % 4, col, extras[n // 4])
        else:
            spread = jnp.where(lane == 64 + 4 * sub + (n - 8), col, spread)
    row = jnp.sum(jnp.where(sub < ROWS, spread, 0.0), axis=0, keepdims=True)
    for h in range(2):
        last_ref[h] = jnp.where(lane8 < 64, extras[h][:8], extras[h][8:])
    last_ref[2] = jnp.broadcast_to(row, (8, 128))


def pack(h, roll_ref, last_ref, o_ref):
    lane = iota((8, 128), 1)
    sub = iota((8, 128), 0)
    for p in range(OWN):
        begin = CH * p + HALF * h
        cut = begin % 128
        here = (lane - cut) & 127
        acc = [None, None]
        for n in range(NB):
            lo = begin + HALF * n
            first, final = lo // 128, (lo + HALF - 1) // 128
            for i in range(2):
                x = roll_ref[n, pl.ds(8 * i, 8), pl.ds(first * 128, 128)]
                if first != final:
                    x = jnp.where(lane >= 64, x, roll_ref[n, pl.ds(8 * i, 8), pl.ds(final * 128, 128)])
                acc[i] = x if n == 0 else jnp.where(here >= HALF * n, x, acc[i])
        low = pltpu.roll(acc[0], 128 - cut, 1) if cut else acc[0]
        high = pltpu.roll(acc[1], (192 - cut) % 128, 1) if cut != 64 else acc[1]
        x = jnp.where(lane < 64, low, high)
        x = jnp.where((lane & 63) >= 60, last_ref[h], x)
        if h:
            x = jnp.where((sub == 7) & (lane >= 64) & (lane < 124), last_ref[2], x)
        o_ref[h, p] = x.astype(BF)


def turn_pieces(h, m_ref, turn_ref):
    for q in range(OWN):
        x = m_ref[h, q].astype(F32)
        cut = (CH * q + HALF * h) % 128
        turn_ref[2 * q + h, pl.ds(0, 8), :] = pltpu.roll(x, cut, 1) if cut else x
        turn_ref[2 * q + h, pl.ds(8, 8), :] = pltpu.roll(x, (cut + 64) % 128, 1) if cut != 64 else x


def unpack(turn_ref, last, c_ref):
    lane = iota((16, 128), 1)
    for n in range(NB):
        tiles = []
        for t in range(6):
            acc = jnp.zeros((16, 128), F32)
            for i in range(2 * OWN):
                a = HALF * (i + n) - t * 128
                if -HALF < a < 128:
                    acc = turn_ref[i] if a <= 0 else jnp.where(lane >= a, turn_ref[i], acc)
            tiles.append(acc)
        full = jnp.concatenate(tiles, axis=1)
        if n:
            full = pltpu.roll(full, 768 - HALF * n, 1)
        c_ref[pl.ds(16 * n, 16), pl.ds(0, 640)] = full[:, :640]
        c_ref[pl.ds(16 * n, 16), pl.ds(640, 128)] = jnp.where(lane == 0, last[:, n : n + 1], 0.0)


def order_matrix():
    out = np.zeros((2, 2, 64, 128), np.float32)
    for h in range(2):
        for half in range(2):
            base = 64 * half
            for g in range(2):
                for n in range(NB):
                    for c in range(2):
                        j = 24 * g + (8 * c + n if n < 8 else 16 + 4 * c + n - 8)
                        out[h, half, j, base + HALF * n + 2 * g + c] = 1
            for n in range(NB):
                j = 48 + n if n < 8 or h else 48 + n + 4
                out[h, half, j, base + HALF * n + 4] = 1
            for t in range(4):
                out[h, half, 60 + t if h else 56 + t, base + 60 + t] = 1
    return out


def row_matrix():
    out = np.zeros((128, 128), np.float32)
    for r in range(ROWS):
        for t in range(4):
            out[8 * r + t, 64 + 4 * r + t] = 1
    return out


def back_matrix():
    out = np.zeros((2, 2, 48, 384), np.float32)
    for h in range(2):
        for half in range(2):
            base = 64 * half
            for n in range(NB):
                for g in range(2):
                    out[h, half, 16 * g + n, base + HALF * n + 2 * g] = 1
                    out[h, half, 16 * g + (n if n < 8 else n + 4), 128 + base + HALF * n + 2 * g + 1] = 1
                out[h, half, 32 + (n if n < 8 or h else n + 4), base + HALF * n + 4] = 1
                out[h, half, 32 + n, 256 + n] = 1
    return out


def sines():
    i = np.arange(192, dtype=np.float64) - R
    return np.sin(np.pi * (i + 0.5) / 180.0).astype(np.float32)[None]


def build_weights(sup_ref, sin_ref, start, t_ref):
    lane = iota((16, 128), 1)
    rlane = lane // 16
    s = lane % 16
    n_in = jnp.where(s < 12, s, s - 4)
    sub = iota((16, 128), 0)
    n_out = jnp.where(sub < 12, sub, sub - 4)
    diff = (n_in - n_out).astype(F32)

    def one(o, carry):
        local = o % 4
        group = o // 4
        row = jnp.minimum(start + o, 179)
        d = rlane - local
        width = jnp.ones((16, 128), F32)
        sine = jnp.zeros((16, 128), F32)
        for j in range(2 * R + 1):
            width = jnp.where(d == j, sup_ref[j, row].astype(F32), width)
            sine = jnp.where(d == j, sin_ref[0, row + j], sine)
        ok = (d >= 0) & (d <= 2 * R)
        scale = jnp.where(ok, sine / jnp.sqrt((2.0 * R + 1.0) * (2.0 * width + 1.0)), 0.0)
        lat = (d - R).astype(F32) / (R + 1.0)
        lat2 = lat * lat
        base = pl.multiple_of(local * 64, 64)
        for step in range(9):
            m = diff + float(12 * (step - 4))
            lon = m / (width + 1.0)
            radius = jnp.sqrt(lat2 + lon * lon) * (K - 1.0)
            w = jnp.where(jnp.abs(m) <= width, scale, 0.0)
            for k in range(K):
                hat = jnp.maximum(0.0, 1.0 - jnp.abs(radius - float(k)))
                t_ref[group, pl.ds(base + 16 * k, 16), pl.ds(128 * step, 128)] = (hat * w).astype(BF)
        return carry

    lax.fori_loop(0, 16, one, 0)


def build_filter(filt_ref, me, w_ref):
    lane = iota((C, 768), 1)
    slot = lane // 64 % 6
    chan = me * CH + HALF * (lane // 384) + slot
    want = jnp.where(slot == 5, C - 1, chan)
    pick = jnp.where(iota((C, 768), 0) == want, 1.0, 0.0).astype(BF)
    w_ref[...] = jnp.dot(filt_ref[...], pick, preferred_element_type=F32)


NT = (((1,), (1,)), ((), ()))
TN = (((0,), (0,)), ((), ()))


def rows_of(x_ref, r):
    return x_ref[pl.ds(r % 8, 64, stride=8), :].astype(BF)


def twice(x):
    return jnp.concatenate([x, x], axis=0)


def turn_rows(h, order_ref, row_ref, parts, last, first, rows, d_ref, e_ref, z_ref):
    if h:
        ex = lax.dot_general(row_ref[...], twice(last), NT, preferred_element_type=F32)
    for i, r in enumerate(rows):
        turned = lax.dot_general(order_ref[h, r // 8], twice(parts[i]), NT, preferred_element_type=F32)
        d_ref[first + i] = turned
        if h:
            e_ref[first + i] = ex[8 * r : 8 * r + 8]
        else:
            z_ref[first + i] = turned[56:64]


def spread_rows(h, start, stop, d_ref, e_ref, z_ref, f_ref):
    lane8 = iota((8, 128), 1)
    sub8 = iota((8, 128), 0)
    left = lane8 < 64
    upper = sub8 < 4
    both = upper == left

    def one(r, carry):
        at = pl.multiple_of(16 * r, 16)
        for step in range(9):
            shift = (4 - step) % 128

            def roll(x):
                return pltpu.roll(x, shift, 1) if shift else x

            turned = roll(d_ref[r])
            for g in range(3):
                if g < 2:
                    top = jnp.where(left, turned[24 * g : 24 * g + 8], turned[24 * g + 8 : 24 * g + 16])
                    low = jnp.where(both, turned[24 * g + 16 : 24 * g + 24], 0.0)
                elif h:
                    tail = turned[56:64]
                    top = jnp.where(left, turned[48:56], jnp.where(upper, roll(z_ref[r]), tail))
                    low = jnp.where(upper, jnp.where(left, tail, roll(e_ref[r])), 0.0)
                else:
                    top = jnp.where(left, turned[48:56], 0.0)
                    low = jnp.where(left & (sub8 >= 4), turned[56:64], 0.0)
                f_ref[step, pl.ds(at, 16), pl.ds(128 * g, 128)] = jnp.concatenate([top, low], axis=0).astype(BF)
        return carry

    lax.fori_loop(start, stop, one, 0)


def convolve(h, groups, t_ref, f_ref, w_ref, back_ref, acc_ref, x_ref, ex_ref):
    for g in groups:
        at = 64 * g
        rhs = jnp.concatenate([f_ref[step, pl.ds(at, 128), :] for step in range(9)], axis=0)
        acc_ref[...] = jnp.dot(t_ref[g], rhs, preferred_element_type=F32)
        for o in range(4):
            conv = jnp.zeros((16, 384), F32)
            for k in range(K):
                conv = conv + acc_ref[pl.ds(64 * o + 16 * k, 16), :] * w_ref[pl.ds(k, 1), pl.ds(384 * h, 384)]
            centre = f_ref[4, pl.ds(at + 16 * (o + R), 16), :].astype(F32)
            comb = (centre + conv).astype(BF)
            stack = jnp.concatenate([comb[:, 128 * i : 128 * i + 128] for i in range(3)], axis=0)
            moved = lax.dot_general(stack, back_ref[h, g // 2], TN, preferred_element_type=F32)
            value = moved[:64, :128] + moved[64:, 128:256]
            row = (4 * g + o) % 8
            if g in (0, 3):
                value = value + x_ref[pl.ds(row, 64, stride=8), :]
            x_ref[pl.ds(row, 64, stride=8), :] = value
            if h:
                ex_ref[4 * g + o] = moved[64:, 256:]


def mlp(c_ref, up_ref, down_ref, out_ref):
    lane = iota((192, 768), 1)
    values = c_ref[...]
    mean = jnp.sum(values, axis=1, keepdims=True) * (1.0 / C)
    centered = jnp.where(lane < C, values - mean, 0.0)
    spread = jnp.sum(centered * centered, axis=1, keepdims=True) * (1.0 / C)
    normed = (centered * lax.rsqrt(spread + 1e-05)).astype(BF)[:, :C]
    raised = jnp.dot(normed, up_ref[...], preferred_element_type=F32)
    hidden = (0.5 * raised * (1.0 + lax.erf(raised * math.sqrt(0.5)))).astype(BF)
    lowered = lax.dot_general(hidden, down_ref[...], NT, preferred_element_type=F32)
    result = (values[:, :C] + lowered).astype(BF)
    for n in range(NB):
        out_ref[n] = result[16 * n : 16 * n + ROWS]


def hail(me, lat, lats, barrier):
    def one(i, carry):
        pl.semaphore_signal(barrier, inc=1, device_id={"lon": lax.rem(me + i, OWN)}, device_id_type=MESH)
        return carry

    lax.fori_loop(1, OWN, one, 0)

    @pl.when(lat > 0)
    def _():
        pl.semaphore_signal(barrier, inc=1, device_id={"lat": lat - 1}, device_id_type=MESH)

    @pl.when(lat < lats - 1)
    def _():
        pl.semaphore_signal(barrier, inc=1, device_id={"lat": lat + 1}, device_id_type=MESH)


def send_all(me, src, dst, send_sem, recv_sem):
    across, along, up = me // 16, me // 8 % 2, me % 8

    def send(i, side):
        p = lax.rem(across + i // 8, 4) * 16 + side * 8 + lax.rem(up + i % 8, 8)
        pltpu.make_async_remote_copy(
            src.at[p], dst.at[me], send_sem, recv_sem, device_id={"lon": p}, device_id_type=MESH
        ).start()

    def far(i, carry):
        send(i, 1 - along)
        return carry

    def near(i, carry):
        send(i, along)
        return carry

    lax.fori_loop(0, 32, far, 0)
    lax.fori_loop(1, 32, near, 0)


def all_sent(me, src, dst, send_sem, recv_sem):
    return pltpu.make_async_remote_copy(
        src.at[pl.ds(0, OWN - 1)], dst.at[pl.ds(0, OWN - 1)], send_sem, recv_sem,
        device_id={"lon": lax.rem(me + 1, OWN)}, device_id_type=MESH,
    )


def kernel(lats, pts_hbm, sup_hbm, sin_hbm, filt_hbm, order_hbm, row_hbm, back_hbm, wup_hbm, wdown_hbm, out_ref,
           sup_ref, sin_ref, filt_ref, order_ref, row_ref, back_ref, pts, wup, wdown, roll_ref, last_ref, msg, own, halo_out, halo_in, t_ref, w_ref, x_ref, d_ref, e_ref, z_ref,
           f_ref, acc_ref, ex_ref, back, pieces, turn_ref, c_ref, load_sem, send_sem, recv_sem, halo_send, halo_recv):
    me = lax.axis_index("lon")
    lat = lax.axis_index("lat")
    barrier = pltpu.get_barrier_semaphore()
    fetch = pltpu.make_async_copy(pts_hbm, pts, load_sem.at[0])
    fetch.start()
    hail(me, lat, lats, barrier)
    fetch_up = pltpu.make_async_copy(wup_hbm, wup, load_sem.at[1])
    fetch_down = pltpu.make_async_copy(wdown_hbm, wdown, load_sem.at[2])
    tables = [
        pltpu.make_async_copy(src, dst, load_sem.at[3 + i])
        for i, (src, dst) in enumerate(
            ((sup_hbm, sup_ref), (sin_hbm, sin_ref), (filt_hbm, filt_ref), (order_hbm, order_ref), (row_hbm, row_ref),
             (back_hbm, back_ref))
        )
    ]
    for copy in tables:
        copy.start()
    fetch_up.start()
    fetch_down.start()
    fetch.wait()
    prepare(pts, roll_ref, last_ref)
    pack(0, roll_ref, last_ref, msg)
    pl.semaphore_wait(barrier, OWN - 1 + (lat > 0).astype(jnp.int32) + (lat < lats - 1).astype(jnp.int32))
    send_all(me, msg.at[0], own.at[0], send_sem.at[0], recv_sem.at[0])
    pack(1, roll_ref, last_ref, msg)
    send_all(me, msg.at[1], own.at[1], send_sem.at[1], recv_sem.at[1])
    for h in range(2):
        own[h, me] = msg[h, me]
    for copy in tables:
        copy.wait()
    build_weights(sup_ref, sin_ref, lat * ROWS, t_ref)
    build_filter(filt_ref, me, w_ref)
    for step in range(9):
        f_ref[step, pl.ds(304, 16), :] = jnp.zeros((16, 384), BF)

    def halo(h, to, i):
        return pltpu.make_async_remote_copy(
            halo_out.at[h, i], halo_in.at[h, i], halo_send.at[h, i], halo_recv.at[h, i],
            device_id={"lat": to}, device_id_type=MESH,
        )

    for h in range(2):
        all_sent(me, msg.at[h], own.at[h], send_sem.at[h], recv_sem.at[h]).wait_recv()
        x_ref[...] = own[h].reshape(512, 128).astype(F32)
        for i, rows in enumerate(((0, 1), (13, 14))):
            for j, r in enumerate(rows):
                halo_out[h, i, j] = rows_of(x_ref, r)
            halo_out[h, i, 2] = rows_of(x_ref, 15)

        @pl.when(lat > 0)
        def _():
            halo(h, lat - 1, 0).start()

        @pl.when(lat < lats - 1)
        def _():
            halo(h, lat + 1, 1).start()

        turn_rows(h, order_ref, row_ref, [rows_of(x_ref, r) for r in range(ROWS)], rows_of(x_ref, 15), R, range(ROWS),
                  d_ref, e_ref, z_ref)
        spread_rows(h, R, ROWS + R, d_ref, e_ref, z_ref, f_ref)
        convolve(h, (1, 2), t_ref, f_ref, w_ref, back_ref, acc_ref, x_ref, ex_ref)

        @pl.when(lat > 0)
        def _():
            halo(h, lat - 1, 1).wait_recv()

        @pl.when(lat == 0)
        def _():
            halo_in[h, 1] = jnp.zeros((3, OWN, 128), BF)

        @pl.when(lat < lats - 1)
        def _():
            halo(h, lat + 1, 0).wait_recv()

        @pl.when(lat == lats - 1)
        def _():
            halo_in[h, 0] = jnp.zeros((3, OWN, 128), BF)

        turn_rows(h, order_ref, row_ref, [halo_in[h, 1, 0], halo_in[h, 1, 1]], halo_in[h, 1, 2], 0, (13, 14),
                  d_ref, e_ref, z_ref)
        turn_rows(h, order_ref, row_ref, [halo_in[h, 0, 0], halo_in[h, 0, 1]], halo_in[h, 0, 2], ROWS + R, (0, 1),
                  d_ref, e_ref, z_ref)
        spread_rows(h, 0, R, d_ref, e_ref, z_ref, f_ref)
        spread_rows(h, ROWS + R, ROWS + 2 * R, d_ref, e_ref, z_ref, f_ref)
        convolve(h, (0, 3), t_ref, f_ref, w_ref, back_ref, acc_ref, x_ref, ex_ref)
        back[h] = x_ref[...].reshape(64, 8, 128).astype(BF)
        send_all(me, back.at[h], pieces.at[h], send_sem.at[2 + h], recv_sem.at[2 + h])
        pieces[h, me] = back[h, me]
    fetch_up.wait()
    fetch_down.wait()
    for h in range(2):
        all_sent(me, msg.at[h], own.at[h], send_sem.at[h], recv_sem.at[h]).wait_send()

        @pl.when(lat > 0)
        def _():
            halo(h, lat - 1, 0).wait_send()

        @pl.when(lat < lats - 1)
        def _():
            halo(h, lat + 1, 1).wait_send()

    last = jnp.concatenate([ex_ref[o, pl.ds(me, 1), :] for o in range(16)], axis=0)
    for h in range(2):
        all_sent(me, back.at[h], pieces.at[h], send_sem.at[2 + h], recv_sem.at[2 + h]).wait_recv()
        turn_pieces(h, pieces, turn_ref)
    unpack(turn_ref, last, c_ref)
    mlp(c_ref, wup, wdown, out_ref)
    for h in range(2):
        all_sent(me, back.at[h], pieces.at[h], send_sem.at[2 + h], recv_sem.at[2 + h]).wait_send()


VM = pl.BlockSpec(memory_space=pltpu.VMEM)
HBM = pl.BlockSpec(memory_space=pltpu.HBM)


def on_device(lats, fields, support, filter_weight, w_up, w_down):
    points = jnp.transpose(fields, (2, 0, 1))
    dma = pltpu.SemaphoreType.DMA
    result = pl.pallas_call(
        functools.partial(kernel, lats), out_shape=jax.ShapeDtypeStruct((NB, ROWS, C), BF),
        in_specs=[HBM] * 9, out_specs=VM,
        scratch_shapes=[
            pltpu.SMEM((5, 180), jnp.int32), pltpu.SMEM((1, 192), F32), pltpu.VMEM((K, C), BF),
            pltpu.VMEM((2, 2, 64, 128), BF), pltpu.VMEM((128, 128), BF), pltpu.VMEM((2, 2, 48, 384), BF),
            pltpu.VMEM((NB, ROWS, C), BF), pltpu.VMEM(w_up.shape, BF), pltpu.VMEM(w_up.shape, BF),
            pltpu.VMEM((NB, 16, 768), F32), pltpu.VMEM((3, 8, 128), F32),
            pltpu.VMEM((2, OWN, 8, 128), BF), pltpu.VMEM((2, OWN, 8, 128), BF),
            pltpu.VMEM((2, 2, 3, OWN, 128), BF), pltpu.VMEM((2, 2, 3, OWN, 128), BF),
            pltpu.VMEM((4, 256, 1152), BF), pltpu.VMEM((K, 768), F32), pltpu.VMEM((512, 128), F32),
            pltpu.VMEM((ROWS + 2 * R, 64, 128), F32), pltpu.VMEM((ROWS + 2 * R, 8, 128), F32),
            pltpu.VMEM((ROWS + 2 * R, 8, 128), F32),
            pltpu.VMEM((9, 320, 384), BF), pltpu.VMEM((256, 384), F32), pltpu.VMEM((16, OWN, 128), F32),
            pltpu.VMEM((2, OWN, 8, 128), BF), pltpu.VMEM((2, OWN, 8, 128), BF),
            pltpu.VMEM((2 * OWN, 16, 128), F32), pltpu.VMEM((192, 768), F32),
            dma((9,)), dma((4,)), dma((4,)), dma((2, 2)), dma((2, 2)),
        ],
        compiler_params=pltpu.CompilerParams(vmem_limit_bytes=40 << 20, collective_id=0, has_side_effects=True),
        name="block",
    )(*(pltpu.with_memory_space_constraint(x, pltpu.HBM) for x in (
        points, support.T, jnp.asarray(sines()), filter_weight.T, jnp.asarray(order_matrix(), BF),
        jnp.asarray(row_matrix(), BF), jnp.asarray(back_matrix(), BF), w_up, w_down.T)))
    return jnp.transpose(result, (1, 2, 0))


def solution(mesh):
    in_specs = (P("lat", None, "lon"), P(), P(), P(), P())
    out_specs = P("lat", None, "lon")
    return jax.shard_map(
        functools.partial(on_device, mesh.shape["lat"]), mesh=mesh, in_specs=in_specs, out_specs=out_specs,
        check_vma=False,
    )
```
